32 devices in a mesh: frame: 8 (over y, x, core), query: 4 (over z).
Axes of the slice: x: 2, y: 2, z: 4, core: 2. Of those that a mesh axis runs over, the one named last changes fastest.
Arguments:
- features: bfloat16 [8, 4096, 256], P('frame'), may hold values from -4.375 to 4.375
- kernel: float32 [3, 3], replicated, may hold values from 0.2 to 1
- cotangent: float32 [2, 8, 4096], P(None, 'frame', 'query'), may hold values from -6 to 6
- query_frame: int32 [4096], P('query'), may hold values from 0 to 7
- query_pixel: int32 [4096], P('query'), may hold values from 0 to 4095
Outputs:
- query_grad: float32 [4096, 256], P('query')
- feature_grad: float32 [8, 4096, 256], P('frame', 'query')
The draws below stay inside these ranges and needn't reach their ends.
All inputs are finite; a program needn't handle non-finite values.
Results may differ from the reference program's by a relative error of at most 0.0029.
Values may be sent and summed in bfloat16 or wider, within the bound.
No kernel may reach another device: no remote copies, remote signals or barrier semaphores. Data moves between devices by JAX's collectives and lax.ppermute only.
A program may use at most 128 MiB of HBM per device.

```python
import math
import jax
import jax.numpy as jnp
import numpy as np
from jax import lax

C = 256
H = 64
W = 64
HW = 4096
T_SIZE = 8
Q = 4096


def draw_features(key, part):
    first = jax.random.fold_in(jax.random.fold_in(key, 11), 0)
    values = jax.random.truncated_normal(first, -6.0, 6.0, (T_SIZE, HW, C), jnp.float32) * C ** (-0.25)
    return values.astype(jnp.bfloat16)


def place_ends(array, stream_key, smallest, high):
    dims = array.shape
    place = [jax.random.randint(jax.random.fold_in(stream_key, axis), (), 0, dims[axis]) for axis in range(len(dims))]
    array = array.at[tuple(place)].set(smallest)
    longest = dims.index(max(dims))
    place[longest] = (place[longest] + 1) % dims[longest]
    return array.at[tuple(place)].set(high)


def block_scale(own_key, dims, shards, low, high):
    level, own = 1.0, jax.random.fold_in(own_key, 6)
    for position, blocks in shards:
        heights = jnp.exp(jax.random.uniform(jax.random.fold_in(own, position), (blocks,), jnp.float32, low / len(shards), high / len(shards)))
        level = level * jnp.repeat(heights, dims[position] // blocks).reshape([-1 if axis == position else 1 for axis in range(len(dims))])
    return level


def rank_table(number_of, skew):
    portions = [(1 << 20) // math.isqrt(standing ** skew) + 1 for standing in range(1, number_of + 1)]
    width = 1 + sum(portions) // (1 << 30)
    return np.cumsum(np.array([max(1, weight // width) for weight in portions]))


def ranked_ids(own_key, shape, amount, skew):
    table = rank_table(amount, skew)
    ticket = jax.random.randint(jax.random.fold_in(own_key, 1), shape, 0, int(table[amount - 1]))
    grade = jnp.searchsorted(jnp.asarray(table, jnp.int32), ticket, side="right")
    return jax.random.permutation(jax.random.fold_in(own_key, 2), amount)[grade].astype(jnp.int32)


def bell_draw(rng, extent, deviation, limit, pieces=(), kind=jnp.bfloat16):
    result = jax.random.normal(rng, extent, jnp.float32) * deviation
    if len(pieces) > 0:
        result = block_scale(rng, extent, pieces, -0.22, 0.18) * result
    return jnp.clip(result, min=-limit, max=limit).astype(kind)


def setup_inputs(seed: int = 0) -> dict:
    splits = jax.random.split(jax.random.key(seed), 6)
    features = draw_features(jax.random.fold_in(splits[5], 71), 0)
    kernel = jnp.clip(jax.random.uniform(splits[1], (3, 3), jnp.float32, 0.2, 1.0), 0.2, 1.0)
    cotangent = bell_draw(splits[2], (2, T_SIZE, Q), 1.0, 6.0, ((1, 8), (2, 4)), jnp.float32)
    query_frame = place_ends(ranked_ids(splits[3], (Q,), T_SIZE, 2), jax.random.fold_in(splits[3], 3), 0, T_SIZE - 1).astype(jnp.int32)
    query_pixel = place_ends(jax.random.randint(splits[4], (Q,), 0, HW), jax.random.fold_in(splits[4], 1), 0, HW - 1).astype(jnp.int32)
    return {"features": features, "kernel": kernel, "cotangent": cotangent, "query_frame": query_frame, "query_pixel": query_pixel}


def conv_fwd(maps, kernel):
    padded = jnp.pad(maps, ((0, 0), (1, 1), (1, 1)))
    total = jnp.zeros_like(maps)
    for a in (-1, 0, 1):
        for b in (-1, 0, 1):
            total = total + kernel[a + 1, b + 1] * padded[:, 1 + a:1 + a + H, 1 + b:1 + b + W]
    return total


def conv_back(maps, kernel):
    padded = jnp.pad(maps, ((0, 0), (1, 1), (1, 1)))
    total = jnp.zeros_like(maps)
    for a in (-1, 0, 1):
        for b in (-1, 0, 1):
            total = total + kernel[a + 1, b + 1] * padded[:, 1 - a:1 - a + H, 1 - b:1 - b + W]
    return total


def reference(features, kernel, cotangent, query_frame, query_pixel):
    qfeat = features[query_frame, query_pixel]
    where_pix = jnp.arange(HW, dtype=jnp.int32)
    row_pos = (where_pix // W).astype(jnp.float32) - (H - 1) / 2.0
    col_pos = (where_pix % W).astype(jnp.float32) - (W - 1) / 2.0

    def one_frame(carry, inputs):
        frame_map, grad_y, grad_x = inputs
        cost = jnp.dot(qfeat, frame_map.T, preferred_element_type=jnp.float32)
        logits = conv_fwd(cost.reshape(Q, H, W), kernel).reshape(Q, HW)
        top = jnp.max(logits, axis=1, keepdims=True)
        expo = jnp.exp(logits - top)
        prob = expo / jnp.sum(expo, axis=1, keepdims=True)
        pull = grad_y[:, None] * row_pos[None, :] + grad_x[:, None] * col_pos[None, :]
        mean_pull = jnp.sum(prob * pull, axis=1, keepdims=True)
        dlogit = prob * (pull - mean_pull)
        dcost = conv_back(dlogit.reshape(Q, H, W), kernel).reshape(Q, HW).astype(jnp.bfloat16)
        carry = carry + jnp.dot(dcost, frame_map, preferred_element_type=jnp.float32)
        frame_grad = jnp.dot(dcost.T, qfeat, preferred_element_type=jnp.float32)
        return carry, frame_grad

    start = jnp.zeros((Q, C), jnp.float32)
    query_grad, frame_grads = lax.scan(one_frame, start, (features, cotangent[0], cotangent[1]))
    flat_rows = query_frame.astype(jnp.int32) * HW + query_pixel.astype(jnp.int32)
    flat_grad = frame_grads.reshape(T_SIZE * HW, C).at[flat_rows].add(query_grad)
    return query_grad, flat_grad.reshape(T_SIZE, HW, C)
```

```python
import functools

import jax
import jax.numpy as jnp
from jax import lax
from jax.experimental import pallas as pl
from jax.experimental.pallas import tpu as pltpu
from jax.sharding import PartitionSpec as P

W = 64
F32 = jnp.float32
BF16 = jnp.bfloat16
NT = (((1,), (1,)), ((), ()))


def dot(a, b):
    return jnp.dot(a, b, preferred_element_type=F32)


def conv_rows(pad_ref, weights, sign, first, count):
    chan = pad_ref.shape[1]
    col = lax.broadcasted_iota(jnp.int32, (W, chan), 0)
    keep_low, keep_high = col >= 1, col <= W - 2
    rows = [
        pad_ref[pl.ds(pl.multiple_of((first + r) * W, W), W), :] for r in range(count + 2)
    ]
    out = []
    for r in range(count):
        taps = {}
        for b in (-1, 0, 1):
            taps[b] = sum(
                weights[sign * a + 1][sign * b + 1] * rows[r + 1 + a] for a in (-1, 0, 1)
            )
        left = jnp.where(keep_low, pltpu.roll(taps[-1], 1, 0), 0.0)
        right = jnp.where(keep_high, pltpu.roll(taps[1], W - 1, 0), 0.0)
        out.append(taps[0] + left + right)
    return jnp.concatenate(out, axis=0)


def load_weights(k_ref):
    return [[k_ref[a, b] for b in range(3)] for a in range(3)]


def prep_kernel(k_ref, f_ref, gh_ref, gl_ref, th_ref, tl_ref, pad_ref):
    pixels, chan = f_ref.shape
    weights = load_weights(k_ref)
    zero = jnp.zeros((W, chan), F32)
    pad_ref[pl.ds(0, W), :] = zero
    pad_ref[pl.ds(pixels + W, W), :] = zero

    def widen(i, c):
        rows = pl.multiple_of(i * 256, 256)
        pad_ref[pl.ds(rows + W, 256), :] = f_ref[pl.ds(rows, 256), :].astype(F32)
        return c

    lax.fori_loop(0, pixels // 256, widen, 0)

    def step(i, c):
        g = conv_rows(pad_ref, weights, 1, i * 4, 4)
        hi = g.astype(BF16)
        at = pl.ds(pl.multiple_of(i * 4 * W, 4 * W), 4 * W)
        gh_ref[at, :] = hi
        gl_ref[at, :] = (g - hi.astype(F32)).astype(BF16)
        t = g.T
        th = t.astype(BF16)
        th_ref[:, at] = th
        tl_ref[:, at] = (t - th.astype(F32)).astype(BF16)
        return c

    lax.fori_loop(0, pixels // (4 * W), step, 0)


def prep(kernel, frame_map):
    pixels, chan = frame_map.shape
    flat = jax.ShapeDtypeStruct((pixels, chan), BF16)
    turned = jax.ShapeDtypeStruct((chan, pixels), BF16)
    vmem = pl.BlockSpec(memory_space=pltpu.VMEM)
    return pl.pallas_call(
        prep_kernel,
        out_shape=(flat, flat, turned, turned),
        in_specs=[pl.BlockSpec(memory_space=pltpu.SMEM), vmem],
        out_specs=(vmem,) * 4,
        scratch_shapes=[pltpu.VMEM((pixels + 2 * W, chan), F32)],
        compiler_params=pltpu.CompilerParams(vmem_limit_bytes=24 << 20),
        cost_estimate=pl.CostEstimate(
            flops=40 * pixels * chan, bytes_accessed=10 * pixels * chan, transcendentals=0
        ),
        name="prep",
    )(kernel, frame_map)


def main_kernel(first, last, *refs):
    k_ref, q_ref, gy_ref, gx_ref, gh_ref, gl_ref, th_ref, tl_ref = refs[:8]
    rest = list(refs[8:])
    yin_ref = None if first else rest.pop(0)
    qg_ref, y_ref, map_ref, acc_ref, qgt_ref = rest
    pixels, chan = gh_ref.shape
    height = pixels // W
    nb = q_ref.shape[0]
    chunk = 8 * W
    step = pl.program_id(0)

    @pl.when(step == 0)
    def _():
        zero = jnp.zeros((W, chan), F32)
        acc_ref[pl.ds(0, W), :] = zero
        acc_ref[pl.ds(pixels + W, W), :] = zero

        def init(i, c):
            rows = pl.multiple_of(i * 256, 256)
            v = jnp.zeros((256, chan), F32) if first else yin_ref[pl.ds(rows, 256), :]
            acc_ref[pl.ds(rows + W, 256), :] = v
            return c

        lax.fori_loop(0, pixels // 256, init, 0)

    q = q_ref[...]

    def logits(i, m):
        at = pl.ds(pl.multiple_of(i * chunk, chunk), chunk)
        l = lax.dot_general(gh_ref[at, :], q, NT, preferred_element_type=F32)
        l += lax.dot_general(gl_ref[at, :], q, NT, preferred_element_type=F32)
        map_ref[at, :] = l
        return jnp.maximum(m, jnp.max(l.reshape(chunk // 8, 8, nb), axis=0))

    m = lax.fori_loop(0, pixels // chunk, logits, jnp.full((8, nb), -jnp.inf, F32))
    m = jnp.max(m, axis=0, keepdims=True)
    mid = (height - 1) / 2.0

    def sums(i, carry):
        cols, ys = carry
        for r in range(4):
            h = i * 4 + r
            at = pl.ds(pl.multiple_of(h * W, W), W)
            e = jnp.exp(map_ref[at, :] - m)
            map_ref[at, :] = e
            ys = ys + jnp.sum(e.reshape(W // 8, 8, nb), axis=0) * (h.astype(F32) - mid)
            cols = cols + e
        return cols, ys

    cols, ys = lax.fori_loop(
        0, height // 4, sums, (jnp.zeros((W, nb), F32), jnp.zeros((8, nb), F32))
    )
    rx = lax.broadcasted_iota(jnp.int32, (W, nb), 0).astype(F32) - (W - 1) / 2.0
    total = jnp.sum(cols, axis=0, keepdims=True)
    ex = jnp.sum(cols * rx, axis=0, keepdims=True)
    ey = jnp.sum(ys, axis=0, keepdims=True)
    inv = 1.0 / total
    gy, gx = gy_ref[...], gx_ref[...]
    mean = (gy * ey + gx * ex) * inv
    u = (gx * rx - mean) * inv
    v = gy * inv

    qgt_ref[...] = jnp.zeros_like(qgt_ref)

    def grads(i, c):
        base = pl.multiple_of(i * chunk, chunk)
        at = pl.ds(base, chunk)
        parts = []
        for r in range(chunk // W):
            h = (i * (chunk // W) + r).astype(F32) - mid
            e = map_ref[pl.ds(base + r * W, W), :]
            parts.append(e * (u + v * h))
        d = jnp.concatenate(parts, axis=0)
        hi = d.astype(BF16)
        lo = (d - hi.astype(F32)).astype(BF16)
        acc_ref[pl.ds(base + W, chunk), :] += dot(hi, q) + dot(lo, q)
        th = th_ref[:, at]
        qgt_ref[...] += dot(th, hi) + dot(tl_ref[:, at], hi) + dot(th, lo)
        return c

    lax.fori_loop(0, pixels // chunk, grads, 0)
    qg_ref[...] = qgt_ref[...].T

    @pl.when(step == pl.num_programs(0) - 1)
    def _():
        if last:
            weights = load_weights(k_ref)

            def back(i, c):
                at = pl.ds(pl.multiple_of(i * 4 * W, 4 * W), 4 * W)
                y_ref[at, :] = conv_rows(acc_ref, weights, -1, i * 4, 4)
                return c

            lax.fori_loop(0, height // 4, back, 0)
        else:

            def copy(i, c):
                rows = pl.multiple_of(i * 256, 256)
                y_ref[pl.ds(rows, 256), :] = acc_ref[pl.ds(rows + W, 256), :]
                return c

            lax.fori_loop(0, pixels // 256, copy, 0)


def main_call(kernel, q, gy, gx, maps, yin, last):
    first = yin is None
    nq, chan = q.shape
    pixels = maps[0].shape[0]
    nb = min(256, nq)

    def whole(shape):
        return pl.BlockSpec(shape, lambda i: (0, 0), pipeline_mode=pl.Buffered(1))

    in_specs = [
        pl.BlockSpec(memory_space=pltpu.SMEM),
        pl.BlockSpec((nb, chan), lambda i: (i, 0)),
        pl.BlockSpec((1, nb), lambda i: (0, i)),
        pl.BlockSpec((1, nb), lambda i: (0, i)),
        whole((pixels, chan)),
        whole((pixels, chan)),
        whole((chan, pixels)),
        whole((chan, pixels)),
    ]
    args = [kernel, q, gy[None, :], gx[None, :], *maps]
    if not first:
        in_specs.append(whole((pixels, chan)))
        args.append(yin)
    return pl.pallas_call(
        functools.partial(main_kernel, first, last),
        grid=(nq // nb,),
        out_shape=(
            jax.ShapeDtypeStruct((nq, chan), F32),
            jax.ShapeDtypeStruct((pixels, chan), F32),
        ),
        in_specs=in_specs,
        out_specs=(
            pl.BlockSpec((nb, chan), lambda i: (i, 0)),
            pl.BlockSpec((pixels, chan), lambda i: (0, 0), pipeline_mode=pl.Buffered(1)),
        ),
        scratch_shapes=[
            pltpu.VMEM((pixels, nb), F32),
            pltpu.VMEM((pixels + 2 * W, chan), F32),
            pltpu.VMEM((chan, nb), F32),
        ],
        compiler_params=pltpu.CompilerParams(
            dimension_semantics=("arbitrary",), vmem_limit_bytes=40 << 20
        ),
        cost_estimate=pl.CostEstimate(
            flops=14 * nq * pixels * chan,
            bytes_accessed=16 * pixels * chan,
            transcendentals=nq * pixels,
        ),
        name="main_last" if last else "main_first",
    )(*args)


def place_kernel(id_ref, rows_ref, out_ref):
    @pl.when(pl.program_id(0) == 0)
    def _():
        out_ref[...] = jnp.zeros_like(out_ref)

    ids = id_ref[...]
    n = ids.shape[1]
    rows = rows_ref[...]
    block = min(256, out_ref.shape[0])
    for b in range(out_ref.shape[0] // block):
        pix = lax.broadcasted_iota(jnp.int32, (block, n), 0) + b * block
        hit = jnp.where(pix == ids, 1.0, 0.0).astype(BF16)
        at = pl.ds(b * block, block)
        out_ref[at, :] += dot(hit, rows)


def place(ids, rows, shard):
    n, chan = rows.shape
    nb = min(512, n)
    return pl.pallas_call(
        place_kernel,
        grid=(n // nb,),
        out_shape=jax.ShapeDtypeStruct((shard, chan), F32),
        in_specs=[
            pl.BlockSpec((1, nb), lambda i: (0, i)),
            pl.BlockSpec((nb, chan), lambda i: (i, 0)),
        ],
        out_specs=pl.BlockSpec((shard, chan), lambda i: (0, 0)),
        compiler_params=pltpu.CompilerParams(
            dimension_semantics=("arbitrary",), vmem_limit_bytes=16 << 20
        ),
        cost_estimate=pl.CostEstimate(
            flops=2 * n * shard * chan, bytes_accessed=2 * n * chan, transcendentals=0
        ),
        name="place",
    )(ids[None, :], rows)


def shards(nf, nz, chunks, features, kernel, cotangent, query_frame, query_pixel):
    _, pixels, chan = features.shape
    nq = query_frame.shape[0]
    half = nf // 2
    rows = nq // nf // chunks
    shard = pixels // nz
    me = lax.axis_index("frame")
    zi = lax.axis_index("query")
    frame_map = features[0]
    order = [2 * i for i in range(half)] + [2 * i + 1 for i in range(half)]

    def fx(v, k):
        return lax.ppermute(v, "frame", [(i, i ^ k) for i in range(nf)])

    def zx(v, k):
        return lax.ppermute(v, "query", [(i, i ^ k) for i in range(nz)])

    owner = me ^ jnp.array(order, jnp.int32)

    def relative(v):
        lead = v.shape[:-1]
        v = v.reshape(*lead, nf, chunks, rows)
        v = jnp.take(v, owner, axis=len(lead))
        return jnp.swapaxes(v, len(lead), len(lead) + 1)

    flat = query_frame * pixels + query_pixel
    flats = jnp.stack([flat] + [zx(flat, k) for k in range(1, nz)])
    ids = relative(flats)
    local = ids[0] - me * pixels
    owned = (local >= 0) & (local < pixels)
    picked = frame_map[jnp.clip(local, 0, pixels - 1).reshape(-1)]
    picked = jnp.where(owned.reshape(-1)[:, None], picked, jnp.zeros((), BF16))
    picked = picked.reshape(chunks, nf, rows, chan)
    pulls = relative(cotangent[:, 0, :]).reshape(2, chunks, nf * rows)
    maps = prep(kernel, frame_map)

    qs = []
    for c in range(chunks):
        mine = picked[c, :half] + fx(picked[c, half:], 1)
        own = mine[0]
        for i in range(1, half):
            own = own + fx(mine[i], 2 * i)
        same = jnp.stack([own] + [fx(own, 2 * i) for i in range(1, half)])
        other = fx(same, 1)
        qs.append(jnp.concatenate([same, other]).reshape(nf * rows, chan))

    yterm = None
    parts = []
    for c in range(chunks):
        qg, yterm = main_call(
            kernel, qs[c], pulls[0, c], pulls[1, c], maps, yterm, c == chunks - 1
        )
        parts.append(qg.reshape(nf, rows, chan))

    pieces = 2
    piece = shard // pieces

    def term(j, p):
        start = jnp.clip(j, 0, nz - 1) * shard + p * piece
        return lax.dynamic_slice_in_dim(yterm, start, piece, axis=0)

    low = [None] * pieces
    high = [None] * pieces
    for t in range(1, nz):
        for p in range(pieces):
            v = term(t - nz + zi, p)
            v = v if low[p] is None else v + low[p].astype(F32)
            low[p] = lax.ppermute(
                v.astype(BF16), "query", [(d, d - 1) for d in range(nz - t, nz)]
            )
            v = term(nz - t + zi, p)
            v = v if high[p] is None else v + high[p].astype(F32)
            high[p] = lax.ppermute(
                v.astype(BF16), "query", [(d, d + 1) for d in range(t)]
            )

    fulls = []
    placed = jnp.zeros((shard, chan), F32)
    base = me * pixels + zi * shard
    for c in range(chunks):
        mine = parts[c][:half] + fx(parts[c][half:], 1)
        own = mine[0]
        for i in range(1, half):
            own = own + fx(mine[i].astype(BF16), 2 * i).astype(F32)
        same = jnp.stack([own] + [fx(own, 2 * i) for i in range(1, half)])
        full = jnp.concatenate([same, fx(same, 1)])
        fulls.append(full)
        narrow = own.astype(BF16)
        others = jnp.stack([zx(narrow, k) for k in range(1, nz)])
        same = jnp.stack([others] + [fx(others, 2 * i) for i in range(1, half)])
        far = jnp.concatenate([same, fx(same, 1)])
        far_ids = jnp.swapaxes(ids[1:, c], 0, 1) - base
        placed = placed + place(
            (ids[0, c] - base).reshape(-1), full.astype(BF16).reshape(-1, chan), shard
        )
        placed = placed + place(far_ids.reshape(-1), far.reshape(-1, chan), shard)

    where = jnp.array([(k // 2) + (k % 2) * half for k in range(nf)], jnp.int32)
    gathered = jnp.stack(fulls, axis=1)
    query_grad = jnp.concatenate(
        [
            lax.dynamic_slice_in_dim(gathered, where[me ^ j], 1, axis=0)
            for j in range(nf)
        ]
    ).reshape(nq, chan)

    mine = lax.dynamic_slice_in_dim(yterm, zi * shard, shard, axis=0)
    arrived = jnp.concatenate(low).astype(F32) + jnp.concatenate(high).astype(F32)
    feature_grad = mine + placed + arrived
    return query_grad, feature_grad[None]


def solution(mesh):
    nf, nz = mesh.shape["frame"], mesh.shape["query"]
    placed = (P("frame", None, None), P(), P(None, "frame", "query"), P("query"), P("query"))
    return jax.shard_map(
        functools.partial(shards, nf, nz, 2),
        mesh=mesh,
        in_specs=placed,
        out_specs=(P("query", None), P("frame", "query", None)),
        check_vma=False,
    )
```

```python
import functools
import math

import jax
import jax.numpy as jnp
from jax import lax
from jax.experimental import pallas as pl
from jax.experimental.pallas import tpu as pltpu
from jax.sharding import PartitionSpec as P

W = 64
LOG2E = math.log2(math.e)
F32 = jnp.float32
BF16 = jnp.bfloat16
NT = (((1,), (1,)), ((), ()))


def dot(a, b):
    return jnp.dot(a, b, preferred_element_type=F32)


def conv_rows(pad_ref, weights, sign, first, count):
    chan = pad_ref.shape[1]
    col = lax.broadcasted_iota(jnp.int32, (W, chan), 0)
    keep_low, keep_high = col >= 1, col <= W - 2
    rows = [
        pad_ref[pl.ds(pl.multiple_of((first + r) * W, W), W), :] for r in range(count + 2)
    ]
    out = []
    for r in range(count):
        taps = {}
        for b in (-1, 0, 1):
            taps[b] = sum(
                weights[sign * a + 1][sign * b + 1] * rows[r + 1 + a] for a in (-1, 0, 1)
            )
        left = jnp.where(keep_low, pltpu.roll(taps[-1], 1, 0), 0.0)
        right = jnp.where(keep_high, pltpu.roll(taps[1], W - 1, 0), 0.0)
        out.append(taps[0] + left + right)
    return jnp.concatenate(out, axis=0)


def load_weights(k_ref):
    return [[k_ref[a, b] for b in range(3)] for a in range(3)]


def prep_kernel(k_ref, f_ref, gg_ref, th_ref, pad_ref):
    pixels, chan = f_ref.shape
    weights = load_weights(k_ref)
    zero = jnp.zeros((W, chan), F32)
    pad_ref[pl.ds(0, W), :] = zero
    pad_ref[pl.ds(pixels + W, W), :] = zero

    def widen(i, c):
        rows = pl.multiple_of(i * 256, 256)
        pad_ref[pl.ds(rows + W, 256), :] = f_ref[pl.ds(rows, 256), :].astype(F32)
        return c

    lax.fori_loop(0, pixels // 256, widen, 0)

    def step(i, c):
        g = conv_rows(pad_ref, weights, 1, i * 4, 4)
        scaled = g * LOG2E
        hi = scaled.astype(BF16)
        at = pl.ds(pl.multiple_of(i * 4 * W, 4 * W), 4 * W)
        gg_ref[at, pl.ds(0, chan)] = hi
        gg_ref[at, pl.ds(chan, chan)] = (scaled - hi.astype(F32)).astype(BF16)
        th_ref[:, at] = g.T.astype(BF16)
        return c

    lax.fori_loop(0, pixels // (4 * W), step, 0, unroll=4)


VMEM = pl.BlockSpec(memory_space=pltpu.VMEM)
SMEM = pl.BlockSpec(memory_space=pltpu.SMEM)


def prep(kernel, frame_map):
    pixels, chan = frame_map.shape
    return pl.pallas_call(
        prep_kernel,
        out_shape=(
            jax.ShapeDtypeStruct((pixels, 2 * chan), BF16),
            jax.ShapeDtypeStruct((chan, pixels), BF16),
        ),
        in_specs=[SMEM, VMEM],
        out_specs=(VMEM, VMEM),
        scratch_shapes=[pltpu.VMEM((pixels + 2 * W, chan), F32)],
        compiler_params=pltpu.CompilerParams(vmem_limit_bytes=12 << 20),
        cost_estimate=pl.CostEstimate(
            flops=40 * pixels * chan, bytes_accessed=10 * pixels * chan, transcendentals=0
        ),
        name="prep",
    )(kernel, frame_map)


def attend_kernel(zero_ref, q_ref, gy_ref, gx_ref, gg_ref, th_ref, *refs):
    (qg_ref, d_ref), scratch = refs[:2], refs[2:]
    pixels = gg_ref.shape[0]
    nb = scratch[0].shape[1]
    blocks = q_ref.shape[0] // nb
    height = pixels // W
    chunk = 4 * W
    steps = pixels // chunk
    mid = (height - 1) / 2.0
    rx = lax.broadcasted_iota(jnp.int32, (W, nb), 0).astype(F32) - (W - 1) / 2.0
    back = pl.multiple_of(zero_ref[0], W)
    maps, exp_ref = scratch[:-1], scratch[-1]

    def lanes(i):
        return pl.ds(i * nb, nb)

    def logits(i, c, m):
        at = pl.ds(c * chunk, chunk)
        q = q_ref[lanes(i), :]
        qq = jnp.concatenate([q, q], axis=1)
        l = lax.dot_general(gg_ref[at, :], qq, NT, preferred_element_type=F32)
        maps[i % len(maps)][at, :] = l
        return jnp.maximum(m, jnp.max(l.reshape(chunk // 8, 8, nb), axis=0))

    def exps(i, c, top, cols, ys):
        for h in range(c * chunk // W, (c + 1) * chunk // W):
            e = jnp.exp2(maps[i % len(maps)][pl.ds(back + h * W, W), :] - top)
            exp_ref[pl.ds(h * W, W), :] = e
            ys = ys + jnp.sum(e.reshape(W // 8, 8, nb), axis=0) * (h - mid)
            cols = cols + e
        return cols, ys

    def stats(i, cols, ys):
        total = jnp.sum(cols, axis=0, keepdims=True)
        ex = jnp.sum(cols * rx, axis=0, keepdims=True)
        ey = jnp.sum(ys, axis=0, keepdims=True)
        inv = 1.0 / total
        gy, gx = gy_ref[:, lanes(i)], gx_ref[:, lanes(i)]
        mean = (gy * ey + gx * ex) * inv
        return (gx * rx - mean) * inv, gy * inv

    low = jnp.full((8, nb), -jnp.inf, F32)
    m = low
    for c in range(steps):
        m = logits(0, c, m)
    for i in range(blocks):
        top = jnp.max(m, axis=0, keepdims=True)
        m, cols, ys = low, jnp.zeros((W, nb), F32), jnp.zeros((8, nb), F32)
        for c in range(steps):
            cols, ys = exps(i, c, top, cols, ys)
            if i + 1 < blocks:
                m = logits(i + 1, c, m)
        u, v = stats(i, cols, ys)
        grad = None
        for g in range(4):
            for h in range(g * height // 4, (g + 1) * height // 4):
                e = exp_ref[pl.ds(back + h * W, W), :]
                d_ref[pl.ds(h * W, W), lanes(i)] = (e * (u + v * (h - mid))).astype(BF16)
            at = pl.ds(g * pixels // 4, pixels // 4)
            part = dot(th_ref[:, at], d_ref[at, lanes(i)])
            grad = part if grad is None else grad + part
        qg_ref[lanes(i), :] = grad.T


def attend(zero, q, gy, gx, gg, th):
    nq, chan = q.shape
    pixels = gg.shape[0]
    nb = min(256, nq)
    return pl.pallas_call(
        attend_kernel,
        out_shape=(
            jax.ShapeDtypeStruct((nq, chan), F32),
            jax.ShapeDtypeStruct((pixels, nq), BF16),
        ),
        in_specs=[SMEM] + [VMEM] * 5,
        out_specs=(VMEM, VMEM),
        scratch_shapes=[pltpu.VMEM((pixels, nb), F32)] * (min(2, nq // nb) + 1),
        compiler_params=pltpu.CompilerParams(vmem_limit_bytes=20 << 20),
        cost_estimate=pl.CostEstimate(
            flops=6 * nq * pixels * chan,
            bytes_accessed=8 * pixels * chan,
            transcendentals=nq * pixels,
        ),
        name="attend",
    )(zero, q, gy, gx, gg, th)


def shard_at(where_ref, nz, hop):
    zi = where_ref[1]
    if hop is None:
        return zi
    level, j = hop
    return jnp.where(zi == nz - level, j, nz - 1 - j)


def feature_kernel(nz, plan, count_d, k_ref, where_ref, *refs):
    pairs = list(zip(refs[:count_d], refs[count_d : 2 * count_d]))
    outs, (y_ref, acc_ref) = refs[2 * count_d : -2], refs[-2:]
    pixels, chan = y_ref.shape
    weights = load_weights(k_ref)
    zero = jnp.zeros((W, chan), F32)
    acc_ref[pl.ds(0, W), :] = zero
    acc_ref[pl.ds(pixels + W, W), :] = zero
    count = 4
    steps = pixels // (count * W)
    ready = [0]

    def product(i):
        at = pl.ds(i * count * W, count * W)
        acc_ref[pl.ds(i * count * W + W, count * W), :] = sum(
            dot(d_ref[at, :], q_ref[...]) for d_ref, q_ref in pairs
        )

    def taps(upto):
        n = upto - ready[0]
        if n > 0:
            y_ref[pl.ds(ready[0] * W, n * W), :] = conv_rows(acc_ref, weights, -1, ready[0], n)
            ready[0] = upto

    for i in range(steps):
        product(i)
        if i > 0:
            taps(i * count - 1)
    taps(steps * count)
    shard = pixels // nz
    for out_ref, (hop, start) in zip(outs, plan):
        base = pl.multiple_of(shard_at(where_ref, nz, hop) * shard + start, 16)
        out_ref[...] = y_ref[pl.ds(base, out_ref.shape[0]), :].astype(out_ref.dtype)


def first_kernel(nz, count_d, k_ref, where_ref, *refs):
    pairs = list(zip(refs[:count_d], refs[count_d : 2 * count_d]))
    outs, (y_ref, acc_ref) = refs[2 * count_d : -2], refs[-2:]
    shard, _ = y_ref.shape
    weights = load_weights(k_ref)
    count = 4
    size = count * W
    top = 2 * where_ref[1] >= nz
    base = jnp.where(top, 0, (nz - 1) * shard)

    def product(start, size):
        at = pl.ds(pl.multiple_of(start, W), size)
        return sum(dot(d_ref[at, :], q_ref[...]) for d_ref, q_ref in pairs)

    edge = product(jnp.where(top, shard, base - W), W)
    acc_ref[pl.ds(0, W), :] = edge * jnp.where(top, 0.0, 1.0)
    acc_ref[pl.ds(shard + W, W), :] = edge * jnp.where(top, 1.0, 0.0)
    done = 0
    for i in range(shard // size):
        acc_ref[pl.ds(i * size + W, size), :] = product(base + i * size, size)
        upto = (i + 1) * count - (1 if (i + 1) * size < shard else 0)
        y_ref[pl.ds(done * W, (upto - done) * W), :] = conv_rows(
            acc_ref, weights, -1, done, upto - done
        )
        done = upto
    start = 0
    for out_ref in outs:
        part = out_ref.shape[0]
        out_ref[...] = y_ref[pl.ds(start, part), :].astype(out_ref.dtype)
        start = (start + part) % shard


def first_terms(kernel, where, nz, cut, ds, qs):
    pixels, chan = ds[0].shape[0], qs[0].shape[1]
    nq = sum(q.shape[0] for q in qs)
    shard = pixels // nz
    sizes = (cut, shard - cut)
    return pl.pallas_call(
        functools.partial(first_kernel, nz, len(ds)),
        out_shape=tuple(
            jax.ShapeDtypeStruct((size, chan), kind) for kind in (BF16, F32) for size in sizes
        ),
        in_specs=[SMEM, SMEM] + [VMEM] * (2 * len(ds)),
        out_specs=(VMEM,) * 4,
        scratch_shapes=[
            pltpu.VMEM((shard, chan), F32),
            pltpu.VMEM((shard + 2 * W, chan), F32),
        ],
        compiler_params=pltpu.CompilerParams(vmem_limit_bytes=8 << 20),
        cost_estimate=pl.CostEstimate(
            flops=2 * nq * shard * chan, bytes_accessed=8 * shard * chan, transcendentals=0
        ),
        name="first",
    )(kernel, where, *ds, *qs)


def feature_terms(kernel, where, nz, hops, ds, qs):
    pixels, chan = ds[0].shape[0], qs[0].shape[1]
    nq = sum(q.shape[0] for q in qs)
    plan = [((level, j), start) for level, j, _, start, _ in hops] + [(None, 0)]
    shapes = [(size, BF16 if level == 1 else F32) for level, _, _, _, size in hops]
    shapes.append((pixels // nz, F32))
    return pl.pallas_call(
        functools.partial(feature_kernel, nz, plan, len(ds)),
        out_shape=tuple(jax.ShapeDtypeStruct((size, chan), kind) for size, kind in shapes),
        in_specs=[SMEM, SMEM] + [VMEM] * (2 * len(ds)),
        out_specs=(VMEM,) * len(shapes),
        scratch_shapes=[
            pltpu.VMEM((pixels, chan), F32),
            pltpu.VMEM((pixels + 2 * W, chan), F32),
        ],
        compiler_params=pltpu.CompilerParams(vmem_limit_bytes=14 << 20),
        cost_estimate=pl.CostEstimate(
            flops=2 * nq * pixels * chan, bytes_accessed=8 * pixels * chan, transcendentals=0
        ),
        name="feature",
    )(kernel, where, *ds, *qs)


def place_kernel(nz, odd, where_ref, *refs):
    ids_refs, rows_ref = refs[:nz], refs[nz]
    half, blocks, rows, chan = rows_ref.shape
    near_ref = refs[nz + 1] if odd else None
    so_far_ref = refs[nz + 2] if odd else None
    out_ref = refs[nz + 3] if odd else refs[nz + 1]
    shard = out_ref.shape[0]
    me, first = where_ref[0], where_ref[2]
    ids = []
    for i in range(half):
        owner = pl.ds(me ^ (2 * i + odd), 1)
        own = ids_refs[0][owner, :]
        ids.append(jnp.concatenate([own, own] + [r[owner, :] for r in ids_refs[1:]], axis=1) - first)
    size = min(256, shard)
    for b in range(shard // size):
        at = pl.ds(b * size, size)
        total = so_far_ref[at, :] if odd else jnp.zeros((size, chan), F32)
        for i in range(half):
            pix = lax.broadcasted_iota(jnp.int32, (size, blocks * rows), 0) + b * size
            hit = jnp.where(pix == ids[i], 1.0, 0.0).astype(BF16)
            total += dot(hit, rows_ref[i].reshape(blocks * rows, chan))
        out_ref[at, :] = total
    if odd:
        grad_ref = refs[nz + 4]
        for i in range(half):
            for k, ref in ((2 * i, near_ref), (2 * i + 1, rows_ref)):
                at = pl.ds(pl.multiple_of((me ^ k) * rows, rows), rows)
                grad_ref[at, :] = ref[i, 0].astype(F32) + ref[i, 1].astype(F32)


def place(where, ids, shard, rows, near=None, so_far=None):
    odd = near is not None
    half, blocks, count, chan = rows.shape
    total = jax.ShapeDtypeStruct((shard, chan), F32)
    grad = jax.ShapeDtypeStruct((2 * half * count, chan), F32)
    args = [where, *ids, rows] + ([near, so_far] if odd else [])
    return pl.pallas_call(
        functools.partial(place_kernel, len(ids), int(odd)),
        out_shape=(total, grad) if odd else total,
        in_specs=[SMEM] + [VMEM] * (len(args) - 1),
        out_specs=(VMEM, VMEM) if odd else VMEM,
        compiler_params=pltpu.CompilerParams(vmem_limit_bytes=12 << 20),
        cost_estimate=pl.CostEstimate(
            flops=2 * half * blocks * count * shard * chan,
            bytes_accessed=4 * shard * chan,
            transcendentals=0,
        ),
        name="place",
    )(*args)


def shards(nf, nz, features, kernel, cotangent, query_frame, query_pixel):
    _, pixels, chan = features.shape
    nq = query_frame.shape[0]
    half = nf // 2
    rows = nq // nf
    shard = pixels // nz
    me = lax.axis_index("frame")
    zi = lax.axis_index("query")
    frame_map = features[0]

    def fx(v, k):
        return lax.ppermute(v, "frame", [(i, i ^ k) for i in range(nf)])

    def zx(v, k):
        return lax.ppermute(v, "query", [(i, i ^ k) for i in range(nz)])

    def swap(v):
        lead = v.shape[:-2]
        bit = 1
        while bit < nf:
            w = v.reshape(*lead, nf // (2 * bit), 2, bit, rows)
            turned = jnp.concatenate([w[..., 1:, :, :], w[..., :1, :, :]], axis=-3)
            v = jnp.where((me & bit) != 0, turned, w).reshape(*lead, nf, rows)
            bit *= 2
        return v

    def relative(v):
        lead = v.shape[:-1]
        v = swap(v.reshape(*lead, nf, rows))
        v = v.reshape(*lead, half, 2, rows)
        return jnp.swapaxes(v, -3, -2).reshape(*lead, nf, rows)

    flat = query_frame * pixels + query_pixel
    local = relative(flat - me * pixels).reshape(-1)
    owned = (local >= 0) & (local < pixels)
    picked = frame_map[jnp.clip(local, 0, pixels - 1)]
    picked = jnp.where(owned[:, None], picked, jnp.zeros((), BF16))
    picked = picked.reshape(nf, rows, chan)
    near, far = nq // 2, nq - nq // 2
    pulls = relative(cotangent[:, 0, :]).reshape(2, nq)
    cuts = [(near, nq), (0, near)]
    pulls = [[pulls[:1, a:b], pulls[1:, a:b]] for a, b in cuts]
    zero = jnp.minimum(zi, 0).astype(jnp.int32)[None]
    where = jnp.stack([me, zi, me * pixels + zi * shard]).astype(jnp.int32)
    flat = flat.reshape(nf, rows)
    frame_map, pulls, where, zero, flat = lax.optimization_barrier(
        (frame_map, pulls, where, zero, flat)
    )
    gg, th = prep(kernel, frame_map)

    mine = picked[:half] + fx(picked[half:], 1)
    mine, flat = lax.optimization_barrier((mine, flat))
    others = [zx(flat, k) for k in range(1, nz)]
    own = mine[0]
    for i in range(1, half):
        own = own + fx(mine[i], 2 * i)
    same = jnp.stack([own] + [fx(own, 2 * i) for i in range(1, half)])
    other = fx(same, 1)
    same, other = same.reshape(near, chan), other.reshape(far, chan)

    far_part, far_d = attend(zero, other, *pulls[0], gg, th)
    crossed = fx(far_part, 1)
    near_part, near_d = attend(zero, same, *pulls[1], gg, th)
    hops = []
    for level in range(1, nz):
        for j in range(nz - level):
            cut = max(16, shard // 2 - 16 * (1 + j % 4))
            if level == 1 and j == nz - 2:
                hops.append((level, j, 0, 0, shard))
            else:
                hops += [(level, j, 0, 0, cut), (level, j, 1, cut, shard - cut)]
    hops.sort(key=lambda h: (h[0] > 1, h[0] + 1.9 * h[1] + 1.1 * h[2]))
    ds, qs = [far_d, near_d], [other, same]
    terms = {}
    firsts = first_terms(kernel, where, nz, hops[0][4], ds, qs)
    terms[1, 0, 0], terms[1, 0, 1], terms[2, 0, 0], terms[2, 0, 1] = firsts
    rest = [h for h in hops if h[:3] not in terms]
    results = feature_terms(kernel, where, nz, rest, ds, qs)
    terms.update({h[:3]: v for h, v in zip(rest, results)})
    came = {}
    for level, j, p, _, _ in hops:
        v = terms[level, j, p]
        if level > 1:
            v = (v + came[level - 1, j, p].astype(F32)).astype(BF16)
        hop = [(nz - level, nz - level - 1), (level - 1, level)]
        came[level, j, p] = lax.ppermute(v, "query", hop)
    arrived = sum(
        jnp.concatenate(
            [came[h[:3]] for h in sorted(hops) if h[0] == level and h[1] == nz - level - 1]
        ).astype(F32)
        for level in range(1, nz)
    )

    mine = (near_part + crossed).reshape(half, rows, chan)
    own = mine[0]
    for i in range(1, half):
        own = own + fx(mine[i], 2 * i)
    upper = own.astype(BF16)
    lower = (own - upper.astype(F32)).astype(BF16)
    known = jnp.stack([upper, lower] + [zx(upper, k) for k in range(1, nz)])
    near = jnp.stack([known] + [fx(known, 2 * i) for i in range(1, half)])
    far = fx(near, 1)
    ids = [flat] + others
    placed = place(where, ids, shard, near)
    placed, query_grad = place(where, ids, shard, far, near, placed)
    feature_grad = results[-1] + arrived + placed
    return query_grad, feature_grad[None]


def solution(mesh):
    nf, nz = mesh.shape["frame"], mesh.shape["query"]
    placed = (P("frame", None, None), P(), P(None, "frame", "query"), P("query"), P("query"))

    def body(*args):
        return shards(nf, nz, *args)

    return jax.shard_map(
        body,
        mesh=mesh,
        in_specs=placed,
        out_specs=(P("query", None), P("frame", "query", None)),
        check_vma=False,
    )
```
